512 devices in a mesh: dp: 16 (over z), retr: 8 (over x, core), fsdp: 4 (over y).
Axes of the slice: x: 4, y: 4, z: 16, core: 2. Of those that a mesh axis runs over, the one named last changes fastest.
Arguments:
- queries: bfloat16 [65536, 2048], P(('dp', 'retr', 'fsdp')), may hold values from -110 to 110, as said below
- encodings: bfloat16 [2048, 128, 896], P(('dp', 'retr', 'fsdp')), may hold values from -6 to 6
- owner_ids: int32 [1024, 2], P(('dp', 'retr', 'fsdp')), may hold values from 0 to 7, all different within a row; in each aligned block of 2 rows (0 to 1, 2 to 3, ...) at most 2 rows name the same one
- local_ids: int32 [1024, 2], P(('dp', 'retr', 'fsdp')), may hold values from 0 to 3
- key_weight: bfloat16 [896, 2048], P(('dp', 'fsdp')), may hold values from -0.1875 to 0.1875
- value_weight: bfloat16 [896, 2048], P(('dp', 'fsdp')), may hold values from -0.1875 to 0.1875
Outputs:
- attended: bfloat16 [65536, 2048], P(('dp', 'retr', 'fsdp'))
The draws below stay inside these ranges and needn't reach their ends.
Inputs may be any that keep to these rules, and one draw needn't show every extreme that they name: `queries`: entries are bounded. `owner_ids`: the two neighbours of a stretch have different owners; among the stretches of one device no owner is named more than 2 times, and in every draw some device's stretches name some owner exactly 2 times.
All inputs are finite; a program needn't handle non-finite values.
Results may differ from the reference program's by a relative error of at most 0.011.
Values may be sent and summed in bfloat16 or wider, within the bound.
No kernel may reach another device: no remote copies, remote signals or barrier semaphores. Data moves between devices by JAX's collectives and lax.ppermute only.
A program may use at most 64 MiB of HBM per device.

```python
import math
import jax
import jax.numpy as jnp
import numpy as np
from jax import lax

HEADS = 16
HS = 128
E = 896
STRETCH = 64
NB = 128
TOK_DEV = 128
PANELS_DEV = 4
MOST = 2
TOKENS = 65536
STRETCHES = 1024
PANELS = 2048
N_RETR = 8
N_FSDP = 4


def draw_queries(key, part):
    first = jax.random.fold_in(key, 0)
    shape = (TOKENS, HEADS * HS)
    return jnp.clip(jax.random.normal(first, shape, jnp.float32), -6.0, 6.0).astype(jnp.bfloat16)


def place_ends(drawn, key, smallest, high):
    dims = drawn.shape
    spot = [jax.random.randint(jax.random.fold_in(key, axis), (), 0, dims[axis]) for axis in range(len(dims))]
    drawn = drawn.at[tuple(spot)].set(smallest)
    longest = dims.index(max(dims))
    spot[longest] = (spot[longest] + 1) % dims[longest]
    return drawn.at[tuple(spot)].set(high)


def steps_of(own_key, dims, shards, least, largest):
    loudness = 1.0
    for position, shards_of in shards:
        draws = jax.random.uniform(jax.random.fold_in(jax.random.fold_in(own_key, 6), position), (shards_of,), jnp.float32, least / len(shards), largest / len(shards))
        loudness = loudness * jnp.repeat(jnp.exp(draws), dims[position] // shards_of).reshape((-1,) + (1,) * (len(dims) - 1 - position))
    return loudness


def shared_out(stream_key, own, number, rows, number_of, top, limit, lean):
    order = jax.random.permutation(stream_key, number_of)
    packed, ordinary = load_shares(number_of, rows * top, limit, lean, True), load_shares(number_of, rows * top, limit, lean, False)
    places = jnp.arange(number_of)

    def named(sizes, offset_by):
        used = int((sizes > 0).sum())
        fixed = max(1, used // 4)
        moved = fixed + (places - fixed + offset_by * (used - fixed)) % max(1, number_of - fixed)
        return jnp.zeros((number_of,), jnp.int32).at[order[jnp.where(places < fixed, places, moved)]].set(jnp.asarray(sizes, jnp.int32))

    sizes = jnp.where(number % 4 == 0, named(packed, number // 4), named(ordinary, number - number // 4 - 1))
    mixed = jax.random.permutation(jax.random.fold_in(own, 3), number_of)
    donor, sink = mixed[0:number_of // 2 * 2:2], mixed[1:number_of // 2 * 2:2]
    room = jnp.minimum(sizes[donor] - 1, limit - sizes[sink]) // 2
    room = jnp.where((donor == order[0]) | (sink == order[0]) | (sizes[sink] == 0), 0, jnp.maximum(room, 0))
    moved = jax.random.randint(jax.random.fold_in(own, 4), (number_of // 2,), 0, 1 << 20) % (room + 1)
    sizes = sizes.at[donor].add(-moved).at[sink].add(moved)
    labels = jnp.searchsorted(jnp.cumsum(sizes), jnp.arange(rows * top), side="right").astype(jnp.int32)
    grid = labels.reshape(top, rows).T
    grid = grid[jax.random.permutation(jax.random.fold_in(own, 1), rows)]
    offset_by = jax.random.randint(jax.random.fold_in(own, 2), (rows, 1), 0, top)
    return jnp.take_along_axis(grid, (jnp.arange(top)[None, :] + offset_by) % top, axis=1)


def load_shares(amount, total, most, skew, full):
    loads = [(1 << 20) // math.isqrt(grade ** skew) + 1 for grade in range(1, amount + 1)]
    largest = most if full else min(most, max(-(-total // amount), total * loads[0] // sum(loads)))
    least = 1 if total - largest >= amount - 1 else 0
    counts, rest = [largest] + [least] * (amount - 1), total - largest - least * (amount - 1)
    while rest > 0:
        movable = [i for i in range(1, amount) if counts[i] < largest] or [i for i in range(1, amount) if counts[i] < most]
        pool, left = sum([loads[i] for i in movable]), rest
        for i in movable:
            addition = min(most - counts[i], max(1, left * loads[i] // pool), rest)
            counts[i] = counts[i] + addition
            rest = rest - addition
    return np.array(counts)


def gaussian(own_key, dims, scale, reach, cuts=(), held_as=jnp.bfloat16):
    factor_of = steps_of(own_key, dims, cuts, -0.22, 0.18) if cuts else 1.0
    values = jax.random.normal(own_key, dims, jnp.float32) * scale * factor_of
    return jnp.minimum(jnp.maximum(values, -reach), reach).astype(held_as)


def setup_inputs(seed: int = 0) -> dict:
    keys = jax.random.split(jax.random.key(seed), 7)
    queries = draw_queries(jax.random.fold_in(keys[6], 71), 0)
    encodings = gaussian(keys[1], (PANELS, NB, E), 1.0, 6.0, ((0, 512),))
    owner_ids_keys = jax.random.split(jax.random.fold_in(keys[2], 1), STRETCHES // (TOK_DEV // STRETCH))
    owner_ids_turns = jax.random.permutation(jax.random.fold_in(keys[2], 3), STRETCHES // (TOK_DEV // STRETCH))
    owner_ids = jax.vmap(lambda own, number: shared_out(jax.random.fold_in(keys[2], 2), own, number, TOK_DEV // STRETCH, N_RETR, 2, MOST, 2))(owner_ids_keys, owner_ids_turns).reshape((STRETCHES, 2))
    local_ids = place_ends(jax.random.randint(keys[3], (STRETCHES, 2), 0, PANELS_DEV), jax.random.fold_in(keys[3], 1), 0, PANELS_DEV - 1).astype(jnp.int32)
    key_weight = gaussian(keys[4], (E, HEADS * HS), E ** -0.5, 0.1875, ((0, 64),))
    value_weight = gaussian(keys[5], (E, HEADS * HS), E ** -0.5, 0.1875, ((0, 64),))
    return dict(queries=queries, encodings=encodings, owner_ids=owner_ids, local_ids=local_ids, key_weight=key_weight, value_weight=value_weight)


def reference(queries, encodings, owner_ids, local_ids, key_weight, value_weight):
    features = HEADS * HS
    stretches_device = TOK_DEV // STRETCH
    stretches_window = stretches_device * N_FSDP
    window = TOK_DEV * N_FSDP
    windows = queries.shape[0] // window
    neighbours = owner_ids.shape[1]

    def one_sequence(sequence):
        sequence = sequence.astype(jnp.int32)
        stretch_ids = sequence * stretches_window + jnp.arange(stretches_window, dtype=jnp.int32)
        device = stretch_ids // stretches_device
        fsdp_index = device % N_FSDP
        data_group = device // (N_RETR * N_FSDP)
        owners = lax.dynamic_slice_in_dim(owner_ids, (sequence * stretches_window).astype(jnp.int32), stretches_window, 0)
        local_rows = lax.dynamic_slice_in_dim(local_ids, (sequence * stretches_window).astype(jnp.int32), stretches_window, 0)
        owner_dev = (data_group[:, None] * N_RETR + owners) * N_FSDP + fsdp_index[:, None]
        panel_ids = (owner_dev * PANELS_DEV + local_rows).astype(jnp.int32)
        panel_rows = jnp.take(encodings, panel_ids.reshape(-1), axis=0).reshape(stretches_window * neighbours * NB, E)
        key_rows = jnp.dot(panel_rows, key_weight, preferred_element_type=jnp.float32).astype(jnp.bfloat16)
        value_rows = jnp.dot(panel_rows, value_weight, preferred_element_type=jnp.float32).astype(jnp.bfloat16)
        key_rows = lax.optimization_barrier(key_rows).astype(jnp.float32)
        value_rows = lax.optimization_barrier(value_rows).astype(jnp.float32)
        query_rows = lax.dynamic_slice_in_dim(queries, (sequence * window).astype(jnp.int32), window, 0)
        shifted = jnp.concatenate([query_rows[STRETCH - 1:], jnp.zeros((STRETCH - 1, features), jnp.bfloat16)], 0)
        query_block = shifted.reshape(stretches_window, STRETCH, HEADS, HS).astype(jnp.float32)
        key_block = key_rows.reshape(stretches_window, neighbours * NB, HEADS, HS)
        value_block = value_rows.reshape(stretches_window, neighbours * NB, HEADS, HS)
        scores = jnp.einsum('cqhd,ckhd->chqk', query_block, key_block) / math.sqrt(HS)
        probs = jax.nn.softmax(scores, axis=-1).astype(jnp.bfloat16)
        probs = lax.optimization_barrier(probs).astype(jnp.float32)
        result = jnp.einsum('chqk,ckhd->cqhd', probs, value_block).astype(jnp.bfloat16)
        result = result.reshape(window, features)
        return jnp.concatenate([jnp.zeros((STRETCH - 1, features), jnp.bfloat16), result[:window - STRETCH + 1]], 0)
    outputs = lax.map(one_sequence, jnp.arange(windows, dtype=jnp.int32))
    return outputs.reshape(windows * window, features)
```

```python
import functools
import math

import jax
import jax.numpy as jnp
from jax import lax
from jax.experimental import pallas as pl
from jax.experimental.pallas import tpu as pltpu
from jax.sharding import PartitionSpec as P

HEADS = 16
STRETCH = 64


def attend_kernel(ids_ref, q_ref, kv_ref, o_ref, *, heads, head_size, stretches, neighbours, scale):
    source = pl.program_id(0)
    columns = heads * head_size
    for j in range(stretches):
        base = (source * stretches + j) * neighbours
        panels = [ids_ref[base + n] for n in range(neighbours)]
        for h in range(heads):
            low = h * head_size
            k = jnp.concatenate([kv_ref[p, :, low : low + head_size] for p in panels], 0)
            v = jnp.concatenate(
                [kv_ref[p, :, columns + low : columns + low + head_size] for p in panels], 0
            )
            q = q_ref[0, j * STRETCH : (j + 1) * STRETCH, low : low + head_size]
            s = (
                lax.dot_general(
                    q, k, (((1,), (1,)), ((), ())), preferred_element_type=jnp.float32
                )
                * scale
            )
            e = jnp.exp(s - jnp.max(s, axis=-1, keepdims=True))
            probs = (e * (1.0 / jnp.sum(e, axis=-1, keepdims=True))).astype(jnp.bfloat16)
            out = jnp.dot(probs, v, preferred_element_type=jnp.float32)
            o_ref[0, j * STRETCH : (j + 1) * STRETCH, low : low + head_size] = out.astype(
                jnp.bfloat16
            )


def spread(block, axis):
    size = lax.axis_size(axis)
    return lax.all_to_all(jnp.broadcast_to(block[None], (size, *block.shape)), axis, 0, 0)


def body(queries, encodings, owner_ids, local_ids, key_weight, value_weight):
    tokens, columns = queries.shape
    stretches = tokens // STRETCH
    neighbours = owner_ids.shape[1]
    group = lax.axis_size("retr")
    mine = columns // group
    head_size = columns // HEADS
    panels = encodings.shape[0]
    width = encodings.shape[2]
    rank = lax.axis_index("retr")
    followers = [(i, i + 1) for i in range(lax.axis_size("fsdp") - 1)]
    leaders = [(i + 1, i) for i in range(lax.axis_size("fsdp") - 1)]

    cut = jnp.concatenate(
        [
            lax.dynamic_slice_in_dim(key_weight, rank * mine, mine, 1),
            lax.dynamic_slice_in_dim(value_weight, rank * mine, mine, 1),
        ],
        1,
    )
    by_dp = spread(cut, "dp")
    by_all = spread(by_dp, "fsdp")
    weight = by_all.transpose(1, 0, 2, 3).reshape(width, 2 * mine)

    late = lax.ppermute(queries[:STRETCH], "fsdp", leaders)
    shifted = jnp.concatenate([queries[STRETCH - 1 :], late[: STRETCH - 1]], 0)
    slots = (owner_ids * panels + local_ids).astype(jnp.bfloat16).reshape(1, 1, stretches * neighbours)
    notes = jnp.pad(
        jnp.broadcast_to(slots, (group, 1, stretches * neighbours)),
        ((0, 0), (0, 15), (0, mine - stretches * neighbours)),
    )
    blocks = shifted.reshape(tokens, group, mine).transpose(1, 0, 2)
    swapped = lax.all_to_all(jnp.concatenate([blocks, notes], 1), "retr", 0, 0)
    ids = swapped[:, tokens, : stretches * neighbours].astype(jnp.int32).reshape(-1)

    everyone = lax.all_gather(encodings, "retr", axis=0, tiled=True)
    kv = jnp.dot(
        everyone.reshape(-1, width), weight, preferred_element_type=jnp.float32
    ).astype(jnp.bfloat16)
    kv = kv.reshape(everyone.shape[0], everyone.shape[1], 2 * mine)

    attended = pl.pallas_call(
        functools.partial(
            attend_kernel,
            heads=mine // head_size,
            head_size=head_size,
            stretches=stretches,
            neighbours=neighbours,
            scale=1.0 / math.sqrt(head_size),
        ),
        out_shape=jax.ShapeDtypeStruct((group, tokens, mine), jnp.bfloat16),
        grid_spec=pltpu.PrefetchScalarGridSpec(
            num_scalar_prefetch=1,
            grid=(group,),
            in_specs=[
                pl.BlockSpec((1, tokens, mine), lambda g, ids: (g, 0, 0)),
                pl.BlockSpec(kv.shape, lambda g, ids: (0, 0, 0)),
            ],
            out_specs=pl.BlockSpec((1, tokens, mine), lambda g, ids: (g, 0, 0)),
        ),
    )(ids, swapped, kv)

    split = tokens - STRETCH
    ahead = lax.ppermute(attended[:, split:], "fsdp", followers)
    ordered = jnp.concatenate([ahead[:, 1:], attended[:, : split + 1]], 1)
    back = lax.all_to_all(ordered, "retr", 0, 0)
    return back.transpose(1, 0, 2).reshape(tokens, columns)


def solution(mesh):
    in_specs = (
        P(("dp", "retr", "fsdp"), None),
        P(("dp", "retr", "fsdp"), None, None),
        P(("dp", "retr", "fsdp"), None),
        P(("dp", "retr", "fsdp"), None),
        P(("dp", "fsdp"), None),
        P(("dp", "fsdp"), None),
    )
    out_specs = P(("dp", "retr", "fsdp"), None)
    return jax.shard_map(body, mesh=mesh, in_specs=in_specs, out_specs=out_specs, check_vma=False)
```
